32 devices in a mesh: energy: 4 (over y, x), slab: 8 (over z, core).
Axes of the slice: x: 2, y: 2, z: 4, core: 2. Of those that a mesh axis runs over, the one named last changes fastest.
Arguments:
- green_init: float32 [32, 8, 2, 128, 128], P('energy', 'slab'), may hold values from -6 to 6
- retarded: float32 [32, 8, 2, 128, 128], P('energy', 'slab'), may hold values from -0.25 to 0.25
- coupling_on: float32 [8, 128, 128], P('slab'), may hold values from -0.5 to 0.5
- coupling_lower: float32 [8, 128, 128], P('slab'), may hold values from -0.5 to 0.5
- coupling_upper: float32 [8, 128, 128], P('slab'), may hold values from -0.5 to 0.5
- phonon_weights: float32 [4], replicated, may hold values from 0.3 to 1
Outputs:
- green_final: float32 [32, 8, 2, 128, 128], P('energy', 'slab')
The draws below stay inside these ranges and needn't reach their ends.
All inputs are finite; a program needn't handle non-finite values.
Results may differ from the reference program's by a relative error of at most 0.0001.
Values sent between devices are 32-bit elements; how exact they have to be, the bound alone decides.
A program may use at most 64 MiB of HBM per device.

```python
import math
import jax
import jax.numpy as jnp
from jax import lax

B = 128
SHIFT_NEAR = 3
SHIFT_FAR = 7
ITERS = 2
ENERGIES = 32
SLABS = 8


def level_of(own_key, shape, pieces, smallest, largest):
    loudness = 1.0
    for axis_at, shards_of in pieces:
        steps = jax.random.uniform(jax.random.fold_in(jax.random.fold_in(own_key, 6), axis_at), (shards_of,), jnp.float32, smallest / len(pieces), largest / len(pieces))
        loudness = loudness * jnp.repeat(jnp.exp(steps), shape[axis_at] // shards_of).reshape((-1,) + (1,) * (len(shape) - 1 - axis_at))
    return loudness


def bell_draw(rng, dims, scale, most, cuts=(), kind=jnp.bfloat16):
    level = level_of(rng, dims, cuts, -0.22, 0.18) if cuts else 1.0
    result = jax.random.normal(rng, dims, jnp.float32) * scale * level
    return jnp.minimum(jnp.maximum(result, -most), most).astype(kind)


def setup_inputs(seed: int = 0) -> dict:
    keys = jax.random.split(jax.random.key(seed), 7)
    green_init = bell_draw(keys[0], (ENERGIES, SLABS, 2, B, B), 1.0, 6.0, ((0, 4), (1, 8)), jnp.float32)
    retarded = bell_draw(keys[1], (ENERGIES, SLABS, 2, B, B), (4 * B) ** -0.5, 0.25, ((0, 4), (1, 8)), jnp.float32)
    coupling_on = bell_draw(keys[2], (SLABS, B, B), B ** -0.5, 0.5, ((0, 8),), jnp.float32)
    coupling_lower = bell_draw(keys[3], (SLABS, B, B), B ** -0.5, 0.5, ((0, 8),), jnp.float32)
    coupling_upper = bell_draw(keys[4], (SLABS, B, B), B ** -0.5, 0.5, ((0, 8),), jnp.float32)
    phonon_weights = jnp.clip(jnp.exp(jax.random.uniform(keys[5], (4,), jnp.float32, math.log(0.3), math.log(1.0))), 0.3, 1.0)
    return {"green_init": green_init, "retarded": retarded, "coupling_on": coupling_on, "coupling_lower": coupling_lower, "coupling_upper": coupling_upper, "phonon_weights": phonon_weights}


HIGH = lax.Precision.HIGHEST


def energy_shift(values, offset):
    total = values.shape[0]
    blank = jnp.zeros_like(values[:abs(offset)])
    if offset > 0:
        return jnp.concatenate([blank, values[:total - offset]], 0)
    return jnp.concatenate([values[-offset:], blank], 0)


def sandwich(coupling, values):
    half_done = jnp.einsum('ij,ecjk->ecik', coupling, values, precision=HIGH)
    return jnp.einsum('ecik,lk->ecil', half_done, coupling, precision=HIGH)


def matmul_plain(left, right):
    return jnp.einsum('eij,ejk->eik', left, right, precision=HIGH)


def matmul_adjoint(left, right):
    return jnp.einsum('eij,ekj->eik', left, right, precision=HIGH)


def propagate(ret_block, self_energy):
    ret_re, ret_im = ret_block[:, 0], ret_block[:, 1]
    sig_re, sig_im = self_energy[:, 0], self_energy[:, 1]
    prod_re = matmul_plain(ret_re, sig_re) - matmul_plain(ret_im, sig_im)
    prod_im = matmul_plain(ret_re, sig_im) + matmul_plain(ret_im, sig_re)
    out_re = matmul_adjoint(prod_re, ret_re) + matmul_adjoint(prod_im, ret_im)
    out_im = matmul_adjoint(prod_im, ret_re) - matmul_adjoint(prod_re, ret_im)
    return jnp.stack([out_re, out_im], 1)


def reference(green_init, retarded, coupling_on, coupling_lower, coupling_upper, phonon_weights):
    offsets = (-SHIFT_FAR, -SHIFT_NEAR, SHIFT_NEAR, SHIFT_FAR)
    current = green_init
    slab_total = current.shape[1]
    for born_step in range(ITERS):
        mixture = phonon_weights[0] * energy_shift(current, offsets[0])
        for which in range(1, 4):
            mixture = mixture + phonon_weights[which] * energy_shift(current, offsets[which])
        padded = jnp.pad(mixture, ((0, 0), (1, 1), (0, 0), (0, 0), (0, 0)))

        def one_slab(slab_index):
            window = lax.dynamic_slice_in_dim(padded, slab_index, 3, 1)
            self_energy = sandwich(coupling_on[slab_index], window[:, 1])
            self_energy = self_energy + sandwich(coupling_lower[slab_index], window[:, 0])
            self_energy = self_energy + sandwich(coupling_upper[slab_index], window[:, 2])
            return propagate(retarded[:, slab_index], self_energy)

        stacked = lax.map(one_slab, jnp.arange(slab_total, dtype=jnp.int32))
        current = jnp.moveaxis(stacked, 0, 1)
    return current
```

```python
import functools

import jax
import jax.numpy as jnp
from jax import lax
from jax.experimental import pallas as pl
from jax.experimental.pallas import tpu as pltpu
from jax.sharding import PartitionSpec as P

SHIFT_NEAR = 3
SHIFT_FAR = 7
ITERS = 2

MESH = pl.DeviceIdType.MESH
F32 = jnp.float32
BF16 = jnp.bfloat16


def split(x):
    hi = x.astype(BF16)
    lo = (x - hi.astype(F32)).astype(BF16)
    return hi, lo


def dot(a, b, rhs_contract=0):
    return lax.dot_general(a, b, (((1,), (rhs_contract,)), ((), ())), preferred_element_type=F32)


def plan(count):
    half = count // 2
    pairs = [[half - 1 - p, half + p] for p in range(half)]
    if count % 2:
        pairs.append([count - 1])
    order = [e for pair in pairs for e in pair]
    first = list(range(half - 1, -1, -1))
    rest = list(range(half, count))
    to_left = [e for e in first + rest if e < SHIFT_FAR]
    mirror = [count - 1 - e for e in first + rest]
    to_right = [e for e in mirror if e >= count - SHIFT_FAR]
    return pairs, to_left, to_right


def kernel(
    counts, weights, green, retarded, c_on, c_low, c_up, out,
    halo, rim, mixed, middle, c_right, c_left, r_left, r_right,
    e_send, e_recv, s_send, s_recv,
):
    n_energy, n_slab = counts
    energies, _, size, _ = green.shape
    d = lax.axis_index("energy")
    s = lax.axis_index("slab")
    pairs, to_left, to_right = plan(energies)
    slot_right = {e: i for i, e in enumerate(to_left)}
    slot_left = {e: i for i, e in enumerate(to_right)}

    has = {("energy", 0): d > 0, ("energy", 1): d < n_energy - 1, ("slab", 0): s > 0, ("slab", 1): s < n_slab - 1}
    at = {"energy": d, "slab": s}
    sides = (0, 1)

    def peer(axis, side):
        return {axis: at[axis] + (1 if side else -1)}

    barrier = pltpu.get_barrier_semaphore()
    for axis in ("energy", "slab"):
        for side in sides:
            @pl.when(has[axis, side])
            def _(axis=axis, side=side):
                pl.semaphore_signal(barrier, inc=1, device_id=peer(axis, side), device_id_type=MESH)
    total = sum(jnp.where(flag, 1, 0) for flag in has.values())
    pl.semaphore_wait(barrier, total)

    def energy_copy(step, side, slot, block):
        return pltpu.make_async_remote_copy(
            src_ref=block, dst_ref=halo.at[step, 1 - side, slot],
            send_sem=e_send.at[step, side, slot], recv_sem=e_recv.at[step, 1 - side, slot],
            device_id=peer("energy", side), device_id_type=MESH,
        )

    def slab_copy(step, side, e):
        return pltpu.make_async_remote_copy(
            src_ref=mixed.at[step, e], dst_ref=rim.at[step, 1 - side, e],
            send_sem=s_send.at[step, side, e], recv_sem=s_recv.at[step, 1 - side, e],
            device_id=peer("slab", side), device_id_type=MESH,
        )

    def held(step):
        return green if step == 0 else middle.at[step - 1]

    def send_energy(step, side, slot):
        e = (to_left, to_right)[side][slot]
        energy_copy(step, side, slot, held(step).at[e]).start()

    @pl.when(has["energy", 0])
    def _():
        for slot in range(len(to_left)):
            send_energy(0, 0, slot)

    @pl.when(has["energy", 1])
    def _():
        for slot in range(len(to_right)):
            send_energy(0, 1, slot)

    for side in sides:
        @pl.when(jnp.logical_not(has["energy", side]))
        def _(side=side):
            halo[:, side] = jnp.zeros_like(halo[:, side])

        @pl.when(jnp.logical_not(has["slab", side]))
        def _(side=side):
            rim[:, side] = jnp.zeros_like(rim[:, side])

    highs, lows = [], []
    for j, ref in enumerate((c_low, c_on, c_up)):
        hi, lo = split(ref[0])
        c_right[j] = jnp.concatenate(
            [jnp.concatenate([hi, hi], 1), jnp.concatenate([lo, lo], 1)], 0)
        highs.append(hi)
        lows.append(lo)
    c_left[...] = jnp.concatenate([jnp.concatenate(highs, 1), jnp.concatenate(lows, 1)], 0)

    @pl.loop(0, energies)
    def _(e):
        re_hi, re_lo = split(retarded[e, 0])
        im_hi, im_lo = split(retarded[e, 1])
        top_hi = jnp.concatenate([re_hi, im_hi], 1)
        top_lo = jnp.concatenate([re_lo, im_lo], 1)
        r_left[e] = jnp.concatenate([top_hi, top_lo], 0)
        r_right[e, 0] = jnp.concatenate([top_hi, jnp.concatenate([-im_hi, re_hi], 1)], 0)
        r_right[e, 1] = jnp.concatenate([top_lo, jnp.concatenate([-im_lo, re_lo], 1)], 0)

    waited = {}

    def wait_halo(step, e):
        need = set()
        for shift in (-SHIFT_FAR, -SHIFT_NEAR, SHIFT_NEAR, SHIFT_FAR):
            at_e = e - shift
            if at_e < 0:
                need.add((0, slot_left[at_e + energies]))
            elif at_e >= energies:
                need.add((1, slot_right[at_e - energies]))
        for side, slot in sorted(need):
            for upto in range(waited.get((step, side), 0), slot + 1):
                @pl.when(has["energy", side])
                def _(side=side, upto=upto):
                    energy_copy(step, 1 - side, upto, held(step).at[0]).wait_recv()
            waited[step, side] = max(waited.get((step, side), 0), slot + 1)

    def part(step, e):
        if e < 0:
            return halo[step, 0, slot_left[e + energies]]
        if e >= energies:
            return halo[step, 1, slot_right[e - energies]]
        return held(step)[e]

    def mix(step, pair):
        for e in pair:
            wait_halo(step, e)
            total = weights[0] * part(step, e + SHIFT_FAR)
            total = total + weights[1] * part(step, e + SHIFT_NEAR)
            total = total + weights[2] * part(step, e - SHIFT_NEAR)
            total = total + weights[3] * part(step, e - SHIFT_FAR)
            mixed[step, e] = total
            for side in sides:
                @pl.when(has["slab", side])
                def _(side=side, e=e):
                    slab_copy(step, side, e).start()

    def two(lhs, rhs, contract):
        both = dot(lhs, rhs[0], contract)
        m = both.shape[0] // 2
        return both[:m] + both[m:] + dot(lhs[:m], rhs[1], contract)

    def solve(step, e):
        for side in sides:
            @pl.when(has["slab", side])
            def _(side=side):
                slab_copy(step, 1 - side, e).wait_recv()
        rights = []
        for j, block in enumerate((rim[step, 0, e], mixed[step, e], rim[step, 1, e])):
            hi, lo = split(block.reshape(2 * size, size))
            half = dot(jnp.concatenate([hi, lo], 1), c_right[j], 1)
            half = half[:, :size] + half[:, size:]
            rights.append(jnp.concatenate([half[:size], half[size:]], 1))
        sigma = two(c_left[...], split(jnp.concatenate(rights, 0)), 0)
        s_hi, s_lo = split(sigma)
        turned = [jnp.concatenate([v, jnp.concatenate([-v[:, size:], v[:, :size]], 1)], 0) for v in (s_hi, s_lo)]
        product = two(r_left[e], turned, 0)
        p_hi, p_lo = split(product)
        result = two(jnp.concatenate([p_hi, p_lo], 0), (r_right[e, 0], r_right[e, 1]), 1)
        target = out if step == ITERS - 1 else middle.at[step]
        target[e, 0] = result[:, :size]
        target[e, 1] = result[:, size:]

    sent = {}

    def pass_on(step, done):
        for side in sides:
            order = (to_left, to_right)[side]
            start = sent.get((step, side), 0)
            stop = start
            while stop < len(order) and order[stop] in done:
                stop += 1
            if stop > start:
                @pl.when(has["energy", side])
                def _(side=side, start=start, stop=stop):
                    for slot in range(start, stop):
                        send_energy(step, side, slot)
            sent[step, side] = stop

    last = len(pairs) - 1
    schedule = [("mix", 0), ("solve", 0)]
    for p in range(1, last + 1):
        schedule.append(("mix", p))
        if p >= 2:
            schedule.append(("solve", p - 1))
    schedule.append(("solve", last))
    if last == 0:
        schedule = [("mix", 0), ("solve", 0)]

    for step in range(ITERS):
        done = set()
        for what, p in schedule:
            if what == "mix":
                mix(step, pairs[p])
            else:
                for e in pairs[p]:
                    solve(step, e)
                done.update(pairs[p])
                if step < ITERS - 1:
                    pass_on(step + 1, done)

    for step in range(ITERS):
        for side in sides:
            @pl.when(has["energy", side])
            def _(side=side):
                for slot in range(len(to_left)):
                    energy_copy(step, side, slot, held(step).at[0]).wait_send()

            @pl.when(has["slab", side])
            def _(side=side):
                for e in range(energies):
                    slab_copy(step, side, e).wait_send()


def solution(mesh):
    counts = (mesh.shape["energy"], mesh.shape["slab"])

    def local(green_init, retarded, coupling_on, coupling_lower, coupling_upper, phonon_weights):
        current = green_init[:, 0]
        local_ret = retarded[:, 0]
        energies, _, size, _ = current.shape
        block = (2, size, size)
        vmem = pl.BlockSpec(memory_space=pltpu.VMEM)
        dma = pltpu.SemaphoreType.DMA
        result = pl.pallas_call(
            functools.partial(kernel, counts),
            out_shape=jax.ShapeDtypeStruct(current.shape, F32),
            in_specs=[pl.BlockSpec(memory_space=pltpu.SMEM)] + [vmem] * 5,
            out_specs=vmem,
            scratch_shapes=[
                pltpu.VMEM((ITERS, 2, SHIFT_FAR) + block, F32),
                pltpu.VMEM((ITERS, 2, energies) + block, F32),
                pltpu.VMEM((ITERS, energies) + block, F32),
                pltpu.VMEM((ITERS - 1, energies) + block, F32),
                pltpu.VMEM((3, 2 * size, 2 * size), BF16),
                pltpu.VMEM((2 * size, 3 * size), BF16),
                pltpu.VMEM((energies, 2 * size, 2 * size), BF16),
                pltpu.VMEM((energies, 2, 2 * size, 2 * size), BF16),
                dma((ITERS, 2, SHIFT_FAR)),
                dma((ITERS, 2, SHIFT_FAR)),
                dma((ITERS, 2, energies)),
                dma((ITERS, 2, energies)),
            ],
            compiler_params=pltpu.CompilerParams(
                collective_id=0, has_side_effects=True, vmem_limit_bytes=48 * 1024 * 1024),
        )(phonon_weights, current, local_ret, coupling_on, coupling_lower, coupling_upper)
        return result[:, None]

    in_specs = (
        P("energy", "slab", None, None, None),
        P("energy", "slab", None, None, None),
        P("slab", None, None),
        P("slab", None, None),
        P("slab", None, None),
        P(),
    )
    out_specs = P("energy", "slab", None, None, None)
    return jax.shard_map(local, mesh=mesh, in_specs=in_specs, out_specs=out_specs, check_vma=False)
```

```python
import functools

import jax
import jax.numpy as jnp
from jax import lax
from jax.experimental import pallas as pl
from jax.experimental.pallas import tpu as pltpu
from jax.sharding import PartitionSpec as P

SHIFT_NEAR = 3
SHIFT_FAR = 7
ITERS = 2

MESH = pl.DeviceIdType.MESH
F32 = jnp.float32
BF16 = jnp.bfloat16


def split(x):
    hi = x.astype(BF16)
    lo = (x - hi.astype(F32)).astype(BF16)
    return hi, lo


def dot(a, b, rhs_contract=0):
    return lax.dot_general(a, b, (((1,), (rhs_contract,)), ((), ())), preferred_element_type=F32)


def needs(e, count):
    found = []
    for shift in (-SHIFT_FAR, -SHIFT_NEAR, SHIFT_NEAR, SHIFT_FAR):
        if e - shift < 0:
            found.append((0, e - shift + count))
        elif e - shift >= count:
            found.append((1, e - shift - count))
    return found


def by_arrival(count, arrivals):
    def ready(e):
        return max([arrivals[side].index(p) for side, p in needs(e, count) if side in arrivals], default=-1)

    order = sorted(range(count), key=lambda e: (ready(e), -e))
    return [order[i:i + 2] for i in range(0, count, 2)]


def inner_first(count):
    half = count // 2
    return list(range(half, count)) + list(range(half - 1, -1, -1))


class Role:
    def __init__(self, when, pairs, arrivals, sends, forwards=None, early=0):
        self.when, self.pairs, self.arrivals = when, pairs, arrivals
        self.sends, self.forwards, self.early = sends, forwards, early
        self.waited, self.sent = {}, {}


def kernel(
    counts, weights, green, retarded, c_on, c_low, c_up, out,
    halo, rim, mixed, middle, c_right, c_left, r_left, r_right,
    e_send, e_recv, s_send, s_recv,
):
    n_energy, n_slab = counts
    energies, _, size, _ = green.shape
    d = lax.axis_index("energy")
    s = lax.axis_index("slab")
    sides = (0, 1)
    has_slab = (s > 0, s < n_slab - 1)
    square = n_energy == 4
    upper = inner_first(energies)
    to_right = [e for e in upper if e >= energies - SHIFT_FAR]
    to_left = [energies - 1 - e for e in to_right]

    if square:
        flip = d >= 2
        is_end = jnp.logical_or(d == 0, d == n_energy - 1)
        is_mid = jnp.logical_not(is_end)
        x_peer = {"energy": d + 1 - 2 * (d % 2)}
        y_peer = {"energy": d + 2 - 4 * (d // 2)}
        peers = [(None, x_peer), (None, y_peer)]
        extra = [e for e in to_left if e not in to_right]
        mid_send = to_right[:2] + extra + to_right[2:]
        end_arrivals = {1: mid_send}
        end_pairs = by_arrival(energies, end_arrivals)
        end_send = [e for pair in end_pairs for e in pair if e >= energies - SHIFT_FAR]
        mid_arrivals = {0: end_send, 1: [energies - 1 - e for e in mid_send if e in to_right]}
        upper_pairs = [[energies - 1 - e, e] for e in upper[:energies // 2]]
        if energies % 2:
            upper_pairs = by_arrival(energies, mid_arrivals)
        roles = [
            Role(is_end, end_pairs, end_arrivals, [(None, x_peer, end_send, 0)], (1, y_peer, to_right), 4),
            Role(is_mid, upper_pairs, mid_arrivals, [(None, x_peer, mid_send, 1)]),
        ]
        empty = [(is_end, 0)]
        have = {}
    else:
        flip = None
        left, right = {"energy": d - 1}, {"energy": d + 1}
        has_left, has_right = d > 0, d < n_energy - 1
        peers = [(has_left, left), (has_right, right)]
        arrivals = {0: to_right, 1: to_left}
        roles = [Role(None, by_arrival(energies, arrivals), arrivals,
                      [(has_left, left, to_left, 1), (has_right, right, to_right, 0)])]
        empty = [(jnp.logical_not(has_left), 0), (jnp.logical_not(has_right), 1)]
        have = {0: has_left, 1: has_right}

    def when(flag, body):
        if flag is None:
            body()
        else:
            pl.when(flag)(body)

    def real(e):
        return e if flip is None else jnp.where(flip, energies - 1 - e, e)

    slabs = [(has_slab[0], {"slab": s - 1}), (has_slab[1], {"slab": s + 1})]
    barrier = pltpu.get_barrier_semaphore()
    total = 0
    for flag, to in peers + slabs:
        def greet(to=to):
            pl.semaphore_signal(barrier, inc=1, device_id=to, device_id_type=MESH)
        when(flag, greet)
        total = total + (1 if flag is None else jnp.where(flag, 1, 0))
    pl.semaphore_wait(barrier, total)

    def held(step, e):
        return green.at[real(e)] if step == 0 else middle.at[step - 1, e]

    def energy_copy(step, lane, src, to, side, slot):
        return pltpu.make_async_remote_copy(
            src_ref=src, dst_ref=halo.at[step, side, slot],
            send_sem=e_send.at[step, lane, slot], recv_sem=e_recv.at[step, side, slot],
            device_id=to, device_id_type=MESH,
        )

    def slab_copy(step, side, e):
        return pltpu.make_async_remote_copy(
            src_ref=mixed.at[step, e], dst_ref=rim.at[step, 1 - side, e],
            send_sem=s_send.at[step, side, e], recv_sem=s_recv.at[step, 1 - side, e],
            device_id=slabs[side][1], device_id_type=MESH,
        )

    def pass_on(role, step, done):
        for lane, (flag, to, order, side) in enumerate(role.sends):
            start = stop = role.sent.get((step, lane), 0)
            while stop < len(order) and order[stop] in done:
                stop += 1

            def send(lane=lane, to=to, todo=order[start:stop], side=side):
                for e in todo:
                    energy_copy(step, lane, held(step, e), to, side, e).start()
            if stop > start:
                when(flag, send)
            role.sent[step, lane] = stop

    def await_halo(role, step, side, upto):
        start = role.waited.get((step, side), 0)
        if upto <= start:
            return
        role.waited[step, side] = upto

        def wait():
            for slot in role.arrivals[side][start:upto]:
                block = halo.at[step, side, slot]
                energy_copy(step, 0, block, peers[0][1], side, slot).wait_recv()
                if role.forwards and role.forwards[0] == side and slot in role.forwards[2]:
                    energy_copy(step, 1, block, role.forwards[1], 1, energies - 1 - slot).start()
        when(have.get(side), wait)

    for role in roles:
        when(role.when, lambda role=role: pass_on(role, 0, range(energies)))

    for flag, side in empty:
        @pl.when(flag)
        def _(side=side):
            halo[:, side] = jnp.zeros_like(halo[:, side])

    for side in sides:
        @pl.when(jnp.logical_not(has_slab[side]))
        def _(side=side):
            rim[:, side] = jnp.zeros_like(rim[:, side])

    highs, lows = [], []
    for j, ref in enumerate((c_low, c_on, c_up)):
        hi, lo = split(ref[0])
        c_right[j] = jnp.concatenate(
            [jnp.concatenate([hi, hi], 1), jnp.concatenate([lo, lo], 1)], 0)
        highs.append(hi)
        lows.append(lo)
    c_left[...] = jnp.concatenate([jnp.concatenate(highs, 1), jnp.concatenate(lows, 1)], 0)

    @pl.loop(0, energies)
    def _(e):
        re_hi, re_lo = split(retarded[real(e), 0])
        im_hi, im_lo = split(retarded[real(e), 1])
        top_hi = jnp.concatenate([re_hi, im_hi], 1)
        top_lo = jnp.concatenate([re_lo, im_lo], 1)
        r_left[e] = jnp.concatenate([top_hi, top_lo], 0)
        r_right[e, 0] = jnp.concatenate([top_hi, jnp.concatenate([-im_hi, re_hi], 1)], 0)
        r_right[e, 1] = jnp.concatenate([top_lo, jnp.concatenate([-im_lo, re_lo], 1)], 0)

    shares = [weights[k] if flip is None else jnp.where(flip, weights[3 - k], weights[k]) for k in range(4)]

    def part(step, e):
        if e < 0:
            return halo[step, 0, e + energies]
        if e >= energies:
            return halo[step, 1, e - energies]
        return held(step, e)[...]

    def mix(role, step, pair):
        for e in pair:
            for side, slot in needs(e, energies):
                if side in role.arrivals:
                    await_halo(role, step, side, role.arrivals[side].index(slot) + 1)
            total = shares[0] * part(step, e + SHIFT_FAR)
            total = total + shares[1] * part(step, e + SHIFT_NEAR)
            total = total + shares[2] * part(step, e - SHIFT_NEAR)
            total = total + shares[3] * part(step, e - SHIFT_FAR)
            mixed[step, e] = total
            for side in sides:
                @pl.when(has_slab[side])
                def _(side=side, e=e):
                    slab_copy(step, side, e).start()

    def two(lhs, rhs, contract):
        both = dot(lhs, rhs[0], contract)
        m = both.shape[0] // 2
        return both[:m] + both[m:] + dot(lhs[:m], rhs[1], contract)

    def solve(step, e):
        for side in sides:
            @pl.when(has_slab[side])
            def _(side=side):
                slab_copy(step, 1 - side, e).wait_recv()
        rights = []
        for j, block in enumerate((rim[step, 0, e], mixed[step, e], rim[step, 1, e])):
            hi, lo = split(block.reshape(2 * size, size))
            half = dot(jnp.concatenate([hi, lo], 1), c_right[j], 1)
            half = half[:, :size] + half[:, size:]
            rights.append(jnp.concatenate([half[:size], half[size:]], 1))
        sigma = two(c_left[...], split(jnp.concatenate(rights, 0)), 0)
        s_hi, s_lo = split(sigma)
        turned = [jnp.concatenate([v, jnp.concatenate([-v[:, size:], v[:, :size]], 1)], 0) for v in (s_hi, s_lo)]
        product = two(r_left[e], turned, 0)
        p_hi, p_lo = split(product)
        result = two(jnp.concatenate([p_hi, p_lo], 0), (r_right[e, 0], r_right[e, 1]), 1)
        target = out.at[real(e)] if step == ITERS - 1 else middle.at[step, e]
        target[0] = result[:, :size]
        target[1] = result[:, size:]

    last = len(roles[0].pairs) - 1
    schedule = [("mix", 0), ("solve", 0)]
    for p in range(1, last + 1):
        schedule.append(("mix", p))
        if p >= 2:
            schedule.append(("solve", p - 1))
    if last:
        schedule.append(("solve", last))

    for step in range(ITERS):
        for what, p in schedule:
            if what == "mix":
                for role in roles:
                    def do_mix(role=role):
                        mix(role, step, role.pairs[p])
                        if p == 0 and role.early:
                            side = role.forwards[0]
                            await_halo(role, step, side, min(role.early, len(role.arrivals[side])))
                    when(role.when, do_mix)
                continue
            for i in range(len(roles[0].pairs[p])):
                e = roles[-1].pairs[p][i]
                if len(roles) > 1:
                    e = jnp.where(roles[0].when, roles[0].pairs[p][i], e)
                solve(step, e)
            if step < ITERS - 1:
                for role in roles:
                    done = [e for pair in role.pairs[:p + 1] for e in pair]
                    when(role.when, lambda role=role, done=done: pass_on(role, step + 1, done))
        for role in roles:
            def rest(role=role):
                for side, order in role.arrivals.items():
                    await_halo(role, step, side, len(order))
            when(role.when, rest)

    for step in range(ITERS):
        for role in roles:
            def finish(role=role):
                for lane, (flag, to, order, side) in enumerate(role.sends):
                    def wait(lane=lane, to=to, order=order, side=side):
                        for e in order:
                            energy_copy(step, lane, held(step, e), to, side, e).wait_send()
                    when(flag, wait)
                if role.forwards:
                    for slot in role.forwards[2]:
                        energy_copy(
                            step, 1, halo.at[step, 1, slot], role.forwards[1], 1, energies - 1 - slot).wait_send()
            when(role.when, finish)
        for side in sides:
            @pl.when(has_slab[side])
            def _(side=side):
                for e in range(energies):
                    slab_copy(step, side, e).wait_send()


def solution(mesh):
    counts = (mesh.shape["energy"], mesh.shape["slab"])

    def local(green_init, retarded, coupling_on, coupling_lower, coupling_upper, phonon_weights):
        current = green_init[:, 0]
        local_ret = retarded[:, 0]
        energies, _, size, _ = current.shape
        block = (2, size, size)
        vmem = pl.BlockSpec(memory_space=pltpu.VMEM)
        dma = pltpu.SemaphoreType.DMA
        result = pl.pallas_call(
            functools.partial(kernel, counts),
            out_shape=jax.ShapeDtypeStruct(current.shape, F32),
            in_specs=[pl.BlockSpec(memory_space=pltpu.SMEM)] + [vmem] * 5,
            out_specs=vmem,
            scratch_shapes=[
                pltpu.VMEM((ITERS, 2, energies) + block, F32),
                pltpu.VMEM((ITERS, 2, energies) + block, F32),
                pltpu.VMEM((ITERS, energies) + block, F32),
                pltpu.VMEM((ITERS - 1, energies) + block, F32),
                pltpu.VMEM((3, 2 * size, 2 * size), BF16),
                pltpu.VMEM((2 * size, 3 * size), BF16),
                pltpu.VMEM((energies, 2 * size, 2 * size), BF16),
                pltpu.VMEM((energies, 2, 2 * size, 2 * size), BF16),
                dma((ITERS, 2, energies)),
                dma((ITERS, 2, energies)),
                dma((ITERS, 2, energies)),
                dma((ITERS, 2, energies)),
            ],
            compiler_params=pltpu.CompilerParams(
                collective_id=0, has_side_effects=True, vmem_limit_bytes=48 * 1024 * 1024),
        )(phonon_weights, current, local_ret, coupling_on, coupling_lower, coupling_upper)
        return result[:, None]

    in_specs = (
        P("energy", "slab", None, None, None),
        P("energy", "slab", None, None, None),
        P("slab", None, None),
        P("slab", None, None),
        P("slab", None, None),
        P(),
    )
    out_specs = P("energy", "slab", None, None, None)
    return jax.shard_map(local, mesh=mesh, in_specs=in_specs, out_specs=out_specs, check_vma=False)
```

```python
import functools

import jax
import jax.numpy as jnp
from jax import lax
from jax.experimental import pallas as pl
from jax.experimental.pallas import tpu as pltpu
from jax.sharding import PartitionSpec as P

SHIFT_NEAR = 3
SHIFT_FAR = 7
ITERS = 2

LAG = 2
POLLS = 2

MESH = pl.DeviceIdType.MESH
F32 = jnp.float32
BF16 = jnp.bfloat16


def split(x):
    hi = x.astype(BF16)
    lo = (x - hi.astype(F32)).astype(BF16)
    return hi, lo


def dot(a, b, rhs_contract=0):
    return lax.dot_general(a, b, (((1,), (rhs_contract,)), ((), ())), preferred_element_type=F32)


def needs(e, count):
    found = []
    for shift in (-SHIFT_FAR, -SHIFT_NEAR, SHIFT_NEAR, SHIFT_FAR):
        if e - shift < 0:
            found.append((0, e - shift + count))
        elif e - shift >= count:
            found.append((1, e - shift - count))
    return found


def by_arrival(count, arrivals, lead=0):
    def ready(e):
        return max(
            [arrivals[side].index(p) - (0 if side else lead) for side, p in needs(e, count) if side in arrivals],
            default=-count)

    return sorted(range(count), key=lambda e: (ready(e), -e))


def inner_first(count):
    half = count // 2
    return list(range(half, count)) + list(range(half - 1, -1, -1))


class Role:
    def __init__(self, when, order, arrivals, sends, forwards=None):
        self.when, self.order, self.arrivals = when, order, arrivals
        self.sends, self.forwards = sends, forwards
        self.waited, self.sent = {}, {}


def kernel(
    counts, weights, green, retarded, c_on, c_low, c_up, out,
    halo, rim, mixed, middle, c_right, c_left, r_left, r_right,
    e_send, e_recv, s_send, s_recv,
):
    n_energy, n_slab = counts
    energies, _, size, _ = green.shape
    d = lax.axis_index("energy")
    s = lax.axis_index("slab")
    sides = (0, 1)
    has_slab = (s > 0, s < n_slab - 1)
    square = n_energy == 4
    upper = inner_first(energies)
    to_right = [e for e in upper if e >= energies - SHIFT_FAR]
    to_left = [energies - 1 - e for e in to_right]

    if square:
        flip = d >= 2
        is_end = jnp.logical_or(d == 0, d == n_energy - 1)
        is_mid = jnp.logical_not(is_end)
        x_peer = {"energy": d + 1 - 2 * (d % 2)}
        y_peer = {"energy": d + 2 - 4 * (d // 2)}
        peers = [(None, x_peer), (None, y_peer)]
        half = energies // 2
        extra = [e for e in to_left if e not in to_right]
        start = to_right[:2] + to_right[-1:] + to_right[2:-1]
        later = [to_right[0]] + to_right[half - 1:half + 1] + to_right[1:half - 1] + to_right[half + 1:]
        mid_send = [start + extra] + [later + extra] * (ITERS - 1)
        end_arrivals = [{1: order} for order in mid_send]
        end_order = [by_arrival(energies, arrivals) for arrivals in end_arrivals]
        end_send = [start] + [[e for e in order if e in to_right] for order in end_order[:-1]]
        mid_arrivals = [
            {0: own, 1: [energies - 1 - e for e in order if e in to_right]}
            for own, order in zip(end_send, mid_send)]
        mid_order = [by_arrival(energies, arrivals, 2.5 if step else 1.5) for step, arrivals in enumerate(mid_arrivals)]
        roles = [
            Role(is_end, end_order, end_arrivals, [(None, x_peer, end_send, 0)], (1, y_peer, to_right)),
            Role(is_mid, mid_order, mid_arrivals, [(None, x_peer, mid_send, 1)]),
        ]
        empty = [(is_end, 0)]
        have = {}
    else:
        flip = None
        left, right = {"energy": d - 1}, {"energy": d + 1}
        has_left, has_right = d > 0, d < n_energy - 1
        peers = [(has_left, left), (has_right, right)]
        arrivals = {0: to_right, 1: to_left}
        every = range(ITERS)
        roles = [Role(
            None, [by_arrival(energies, arrivals) for _ in every], [arrivals for _ in every],
            [(has_left, left, [to_left for _ in every], 1), (has_right, right, [to_right for _ in every], 0)])]
        empty = [(jnp.logical_not(has_left), 0), (jnp.logical_not(has_right), 1)]
        have = {0: has_left, 1: has_right}

    def when(flag, body):
        if flag is None:
            body()
        else:
            pl.when(flag)(body)

    def real(e):
        return e if flip is None else jnp.where(flip, energies - 1 - e, e)

    slabs = [(has_slab[0], {"slab": s - 1}), (has_slab[1], {"slab": s + 1})]
    barrier = pltpu.get_barrier_semaphore()
    total = 0
    for flag, to in peers + slabs:
        def greet(to=to):
            pl.semaphore_signal(barrier, inc=1, device_id=to, device_id_type=MESH)
        when(flag, greet)
        total = total + (1 if flag is None else jnp.where(flag, 1, 0))
    pl.semaphore_wait(barrier, total)

    def held(step, e):
        return green.at[real(e)] if step == 0 else middle.at[step - 1, e]

    def energy_copy(step, lane, src, to, side, slot):
        return pltpu.make_async_remote_copy(
            src_ref=src, dst_ref=halo.at[step, side, slot],
            send_sem=e_send.at[step, lane, slot], recv_sem=e_recv.at[step, side, slot],
            device_id=to, device_id_type=MESH,
        )

    def slab_copy(step, side, e):
        return pltpu.make_async_remote_copy(
            src_ref=mixed.at[step, e], dst_ref=rim.at[step, 1 - side, e],
            send_sem=s_send.at[step, side, e], recv_sem=s_recv.at[step, 1 - side, e],
            device_id=slabs[side][1], device_id_type=MESH,
        )

    def pass_on(role, step, done):
        for lane, (flag, to, orders, side) in enumerate(role.sends):
            order = orders[step]
            start = stop = role.sent.get((step, lane), 0)
            while stop < len(order) and order[stop] in done:
                stop += 1

            def send(lane=lane, to=to, todo=order[start:stop], side=side):
                for e in todo:
                    energy_copy(step, lane, held(step, e), to, side, e).start()
            if stop > start:
                when(flag, send)
            role.sent[step, lane] = stop

    def await_halo(role, step, side, upto):
        start = role.waited.get((step, side), 0)
        if upto <= start:
            return
        role.waited[step, side] = upto

        def wait():
            for slot in role.arrivals[step][side][start:upto]:
                block = halo.at[step, side, slot]
                energy_copy(step, 0, block, peers[0][1], side, slot).wait_recv()
                if role.forwards and role.forwards[0] == side and slot in role.forwards[2]:
                    energy_copy(step, 1, block, role.forwards[1], 1, energies - 1 - slot).start()
        when(have.get(side), wait)

    for role in roles:
        when(role.when, lambda role=role: pass_on(role, 0, range(energies)))

    for flag, side in empty:
        @pl.when(flag)
        def _(side=side):
            halo[:, side] = jnp.zeros_like(halo[:, side])

    for side in sides:
        @pl.when(jnp.logical_not(has_slab[side]))
        def _(side=side):
            rim[:, side] = jnp.zeros_like(rim[:, side])

    highs, lows = [], []
    for j, ref in enumerate((c_low, c_on, c_up)):
        hi, lo = split(ref[0])
        c_right[j] = jnp.concatenate(
            [jnp.concatenate([hi, hi], 1), jnp.concatenate([lo, lo], 1)], 0)
        highs.append(hi)
        lows.append(lo)
    c_left[...] = jnp.concatenate([jnp.concatenate(highs, 1), jnp.concatenate(lows, 1)], 0)

    @pl.loop(0, energies)
    def _(e):
        re_hi, re_lo = split(retarded[real(e), 0])
        im_hi, im_lo = split(retarded[real(e), 1])
        top_hi = jnp.concatenate([re_hi, im_hi], 1)
        top_lo = jnp.concatenate([re_lo, im_lo], 1)
        r_left[e] = jnp.concatenate([top_hi, top_lo], 0)
        r_right[e, 0] = jnp.concatenate([top_hi, jnp.concatenate([-im_hi, re_hi], 1)], 0)
        r_right[e, 1] = jnp.concatenate([top_lo, jnp.concatenate([-im_lo, re_lo], 1)], 0)

    shares = [weights[k] if flip is None else jnp.where(flip, weights[3 - k], weights[k]) for k in range(4)]

    def part(step, e):
        if e < 0:
            return halo[step, 0, e + energies]
        if e >= energies:
            return halo[step, 1, e - energies]
        return held(step, e)[...]

    def mix(role, step, e):
        for side, slot in needs(e, energies):
            if side in role.arrivals[step]:
                await_halo(role, step, side, role.arrivals[step][side].index(slot) + 1)
        total = shares[0] * part(step, e + SHIFT_FAR)
        total = total + shares[1] * part(step, e + SHIFT_NEAR)
        total = total + shares[2] * part(step, e - SHIFT_NEAR)
        total = total + shares[3] * part(step, e - SHIFT_FAR)
        mixed[step, e] = total
        for side in sides:
            @pl.when(has_slab[side])
            def _(side=side):
                slab_copy(step, side, e).start()

    def two(lhs, rhs, contract):
        both = dot(lhs, rhs[0], contract)
        m = both.shape[0] // 2
        return both[:m] + both[m:] + dot(lhs[:m], rhs[1], contract)

    def solve(step, e):
        for side in sides:
            @pl.when(has_slab[side])
            def _(side=side):
                slab_copy(step, 1 - side, e).wait_recv()
        rights = []
        for j, block in enumerate((rim[step, 0, e], mixed[step, e], rim[step, 1, e])):
            hi, lo = split(block.reshape(2 * size, size))
            half = dot(jnp.concatenate([hi, lo], 1), c_right[j], 1)
            half = half[:, :size] + half[:, size:]
            rights.append(jnp.concatenate([half[:size], half[size:]], 1))
        sigma = two(c_left[...], split(jnp.concatenate(rights, 0)), 0)
        s_hi, s_lo = split(sigma)
        turned = [jnp.concatenate([v, jnp.concatenate([-v[:, size:], v[:, :size]], 1)], 0) for v in (s_hi, s_lo)]
        product = two(r_left[e], turned, 0)
        p_hi, p_lo = split(product)
        result = two(jnp.concatenate([p_hi, p_lo], 0), (r_right[e, 0], r_right[e, 1]), 1)
        target = out.at[real(e)] if step == ITERS - 1 else middle.at[step, e]
        target[0] = result[:, :size]
        target[1] = result[:, size:]

    for step in range(ITERS):
        for i in range(energies + LAG):
            if i < energies:
                for role in roles:
                    when(role.when, lambda role=role: mix(role, step, role.order[step][i]))
            at = i - LAG
            if at < 0:
                continue
            ahead = at - energies + POLLS + 1
            if step < ITERS - 1 and ahead > 0:
                for role in roles:
                    if role.forwards:
                        side = role.forwards[0]
                        when(role.when, lambda: await_halo(
                            role, step + 1, side, min(ahead, len(role.arrivals[step + 1][side]))))
            e = roles[-1].order[step][at]
            if len(roles) > 1:
                e = jnp.where(roles[0].when, roles[0].order[step][at], e)
            solve(step, e)
            if step < ITERS - 1:
                for role in roles:
                    when(role.when, lambda role=role: pass_on(role, step + 1, role.order[step][:at + 1]))
        for role in roles:
            def rest(role=role):
                for side, order in role.arrivals[step].items():
                    await_halo(role, step, side, len(order))
            when(role.when, rest)

    for step in range(ITERS):
        for role in roles:
            def finish(role=role):
                for lane, (flag, to, orders, side) in enumerate(role.sends):
                    def wait(lane=lane, to=to, order=orders[step], side=side):
                        for e in order:
                            energy_copy(step, lane, held(step, e), to, side, e).wait_send()
                    when(flag, wait)
                if role.forwards:
                    for slot in role.forwards[2]:
                        energy_copy(
                            step, 1, halo.at[step, 1, slot], role.forwards[1], 1, energies - 1 - slot).wait_send()
            when(role.when, finish)
        for side in sides:
            @pl.when(has_slab[side])
            def _(side=side):
                for e in range(energies):
                    slab_copy(step, side, e).wait_send()


def solution(mesh):
    counts = (mesh.shape["energy"], mesh.shape["slab"])

    def local(green_init, retarded, coupling_on, coupling_lower, coupling_upper, phonon_weights):
        current = green_init[:, 0]
        local_ret = retarded[:, 0]
        energies, _, size, _ = current.shape
        block = (2, size, size)
        vmem = pl.BlockSpec(memory_space=pltpu.VMEM)
        dma = pltpu.SemaphoreType.DMA
        result = pl.pallas_call(
            functools.partial(kernel, counts),
            out_shape=jax.ShapeDtypeStruct(current.shape, F32),
            in_specs=[pl.BlockSpec(memory_space=pltpu.SMEM)] + [vmem] * 5,
            out_specs=vmem,
            scratch_shapes=[
                pltpu.VMEM((ITERS, 2, energies) + block, F32),
                pltpu.VMEM((ITERS, 2, energies) + block, F32),
                pltpu.VMEM((ITERS, energies) + block, F32),
                pltpu.VMEM((ITERS - 1, energies) + block, F32),
                pltpu.VMEM((3, 2 * size, 2 * size), BF16),
                pltpu.VMEM((2 * size, 3 * size), BF16),
                pltpu.VMEM((energies, 2 * size, 2 * size), BF16),
                pltpu.VMEM((energies, 2, 2 * size, 2 * size), BF16),
                dma((ITERS, 2, energies)),
                dma((ITERS, 2, energies)),
                dma((ITERS, 2, energies)),
                dma((ITERS, 2, energies)),
            ],
            compiler_params=pltpu.CompilerParams(
                collective_id=0, has_side_effects=True, vmem_limit_bytes=48 * 1024 * 1024),
        )(phonon_weights, current, local_ret, coupling_on, coupling_lower, coupling_upper)
        return result[:, None]

    in_specs = (
        P("energy", "slab", None, None, None),
        P("energy", "slab", None, None, None),
        P("slab", None, None),
        P("slab", None, None),
        P("slab", None, None),
        P(),
    )
    out_specs = P("energy", "slab", None, None, None)
    return jax.shard_map(local, mesh=mesh, in_specs=in_specs, out_specs=out_specs, check_vma=False)
```

```python
import functools

import jax
import jax.numpy as jnp
from jax import lax
from jax.experimental import pallas as pl
from jax.experimental.pallas import tpu as pltpu
from jax.sharding import PartitionSpec as P

SHIFT_NEAR = 3
SHIFT_FAR = 7
ITERS = 2

LAG = 2
POLLS = 2

MESH = pl.DeviceIdType.MESH
F32 = jnp.float32
BF16 = jnp.bfloat16


def split(x):
    hi = x.astype(BF16)
    lo = (x - hi.astype(F32)).astype(BF16)
    return hi, lo


def dot(a, b, rhs_contract=0):
    return lax.dot_general(a, b, (((1,), (rhs_contract,)), ((), ())), preferred_element_type=F32)


def needs(e, count):
    found = []
    for shift in (-SHIFT_FAR, -SHIFT_NEAR, SHIFT_NEAR, SHIFT_FAR):
        if e - shift < 0:
            found.append((0, e - shift + count))
        elif e - shift >= count:
            found.append((1, e - shift - count))
    return found


def by_arrival(count, arrivals, lead=0):
    def ready(e):
        return max(
            [arrivals[side].index(p) - (0 if side else lead) for side, p in needs(e, count) if side in arrivals],
            default=-count)

    return sorted(range(count), key=lambda e: (ready(e), -e))


def inner_first(count):
    half = count // 2
    return list(range(half, count)) + list(range(half - 1, -1, -1))


class Role:
    def __init__(self, when, order, arrivals, sends, forwards=None):
        self.when, self.order, self.arrivals = when, order, arrivals
        self.sends, self.forwards = sends, forwards
        self.waited, self.sent = {}, {}


def kernel(
    counts, weights_in, green_in, retarded_in, on_in, low_in, up_in, out_hbm,
    weights, green, retarded, c_on, c_low, c_up, out, load_sem, store_sem,
    halo, rim, mixed, middle, c_right, c_left, r_left, r_right,
    e_send, e_recv, s_send, s_recv,
):
    n_energy, n_slab = counts
    energies, _, size, _ = green.shape
    d = lax.axis_index("energy")
    s = lax.axis_index("slab")
    sides = (0, 1)
    has_slab = (s > 0, s < n_slab - 1)
    square = n_energy == 4
    upper = inner_first(energies)
    to_right = [e for e in upper if e >= energies - SHIFT_FAR]
    to_left = [energies - 1 - e for e in to_right]

    if square:
        flip = d >= 2
        is_end = jnp.logical_or(d == 0, d == n_energy - 1)
        is_mid = jnp.logical_not(is_end)
        x_peer = {"energy": d + 1 - 2 * (d % 2)}
        y_peer = {"energy": d + 2 - 4 * (d // 2)}
        peers = [(None, x_peer), (None, y_peer)]
        half = energies // 2
        extra = [e for e in to_left if e not in to_right]
        start = to_right[:2] + to_right[-1:] + to_right[2:-1]
        later = [to_right[0]] + to_right[half - 1:half + 1] + to_right[1:half - 1] + to_right[half + 1:]
        mid_send = [start + extra] + [later + extra] * (ITERS - 1)
        end_arrivals = [{1: order} for order in mid_send]
        end_order = [by_arrival(energies, arrivals) for arrivals in end_arrivals]
        end_send = [start] + [[e for e in order if e in to_right] for order in end_order[:-1]]
        mid_arrivals = [
            {0: own, 1: [energies - 1 - e for e in order if e in to_right]}
            for own, order in zip(end_send, mid_send)]
        mid_order = [by_arrival(energies, arrivals, 2.5 if step else 1.5) for step, arrivals in enumerate(mid_arrivals)]
        roles = [
            Role(is_end, end_order, end_arrivals, [(None, x_peer, end_send, 0)], (1, y_peer, to_right)),
            Role(is_mid, mid_order, mid_arrivals, [(None, x_peer, mid_send, 1)]),
        ]
        empty = [(is_end, 0)]
        have = {}
    else:
        flip = None
        left, right = {"energy": d - 1}, {"energy": d + 1}
        has_left, has_right = d > 0, d < n_energy - 1
        peers = [(has_left, left), (has_right, right)]
        arrivals = {0: to_right, 1: to_left}
        every = range(ITERS)
        roles = [Role(
            None, [by_arrival(energies, arrivals) for _ in every], [arrivals for _ in every],
            [(has_left, left, [to_left for _ in every], 1), (has_right, right, [to_right for _ in every], 0)])]
        empty = [(jnp.logical_not(has_left), 0), (jnp.logical_not(has_right), 1)]
        have = {0: has_left, 1: has_right}

    def when(flag, body):
        if flag is None:
            body()
        else:
            pl.when(flag)(body)

    def real(e):
        return e if flip is None else jnp.where(flip, energies - 1 - e, e)

    loads = [
        pltpu.make_async_copy(src, dst, load_sem.at[i])
        for i, (src, dst) in enumerate((
            (low_in, c_low), (on_in, c_on), (up_in, c_up), (retarded_in, retarded),
            (weights_in, weights), (green_in, green)))]

    slabs = [(has_slab[0], {"slab": s - 1}), (has_slab[1], {"slab": s + 1})]
    barrier = pltpu.get_barrier_semaphore()
    total = 0
    for flag, to in peers + slabs:
        def greet(to=to):
            pl.semaphore_signal(barrier, inc=1, device_id=to, device_id_type=MESH)
        when(flag, greet)
        total = total + (1 if flag is None else jnp.where(flag, 1, 0))
    pl.semaphore_wait(barrier, total)

    def held(step, e):
        return green.at[real(e)] if step == 0 else middle.at[step - 1, e]

    def source(step, e):
        return green_in.at[real(e)] if step == 0 else middle.at[step - 1, e]

    def energy_copy(step, lane, src, to, side, slot):
        return pltpu.make_async_remote_copy(
            src_ref=src, dst_ref=halo.at[step, side, slot],
            send_sem=e_send.at[step, lane, slot], recv_sem=e_recv.at[step, side, slot],
            device_id=to, device_id_type=MESH,
        )

    def slab_copy(step, side, e):
        return pltpu.make_async_remote_copy(
            src_ref=mixed.at[step, e], dst_ref=rim.at[step, 1 - side, e],
            send_sem=s_send.at[step, side, e], recv_sem=s_recv.at[step, 1 - side, e],
            device_id=slabs[side][1], device_id_type=MESH,
        )

    def pass_on(role, step, done):
        for lane, (flag, to, orders, side) in enumerate(role.sends):
            order = orders[step]
            start = stop = role.sent.get((step, lane), 0)
            while stop < len(order) and order[stop] in done:
                stop += 1

            def send(lane=lane, to=to, todo=order[start:stop], side=side):
                for e in todo:
                    energy_copy(step, lane, source(step, e), to, side, e).start()
            if stop > start:
                when(flag, send)
            role.sent[step, lane] = stop

    def await_halo(role, step, side, upto):
        start = role.waited.get((step, side), 0)
        if upto <= start:
            return
        role.waited[step, side] = upto

        def wait():
            for slot in role.arrivals[step][side][start:upto]:
                block = halo.at[step, side, slot]
                energy_copy(step, 0, block, peers[0][1], side, slot).wait_recv()
                if role.forwards and role.forwards[0] == side and slot in role.forwards[2]:
                    energy_copy(step, 1, block, role.forwards[1], 1, energies - 1 - slot).start()
        when(have.get(side), wait)

    for role in roles:
        when(role.when, lambda role=role: pass_on(role, 0, range(energies)))

    for load in loads:
        load.start()

    for flag, side in empty:
        @pl.when(flag)
        def _(side=side):
            halo[:, side] = jnp.zeros_like(halo[:, side])

    for side in sides:
        @pl.when(jnp.logical_not(has_slab[side]))
        def _(side=side):
            rim[:, side] = jnp.zeros_like(rim[:, side])

    for load in loads[:3]:
        load.wait()
    highs, lows = [], []
    for j, ref in enumerate((c_low, c_on, c_up)):
        hi, lo = split(ref[0])
        c_right[j] = jnp.concatenate(
            [jnp.concatenate([hi, hi], 1), jnp.concatenate([lo, lo], 1)], 0)
        highs.append(hi)
        lows.append(lo)
    c_left[...] = jnp.concatenate([jnp.concatenate(highs, 1), jnp.concatenate(lows, 1)], 0)

    loads[3].wait()

    @pl.loop(0, energies)
    def _(e):
        re_hi, re_lo = split(retarded[real(e), 0])
        im_hi, im_lo = split(retarded[real(e), 1])
        top_hi = jnp.concatenate([re_hi, im_hi], 1)
        top_lo = jnp.concatenate([re_lo, im_lo], 1)
        r_left[e] = jnp.concatenate([top_hi, top_lo], 0)
        r_right[e, 0] = jnp.concatenate([top_hi, jnp.concatenate([-im_hi, re_hi], 1)], 0)
        r_right[e, 1] = jnp.concatenate([top_lo, jnp.concatenate([-im_lo, re_lo], 1)], 0)

    for load in loads[4:]:
        load.wait()
    shares = [weights[k] if flip is None else jnp.where(flip, weights[3 - k], weights[k]) for k in range(4)]

    def part(step, e):
        if e < 0:
            return halo[step, 0, e + energies]
        if e >= energies:
            return halo[step, 1, e - energies]
        return held(step, e)[...]

    def mix(role, step, e):
        for side, slot in needs(e, energies):
            if side in role.arrivals[step]:
                await_halo(role, step, side, role.arrivals[step][side].index(slot) + 1)
        total = shares[0] * part(step, e + SHIFT_FAR)
        total = total + shares[1] * part(step, e + SHIFT_NEAR)
        total = total + shares[2] * part(step, e - SHIFT_NEAR)
        total = total + shares[3] * part(step, e - SHIFT_FAR)
        mixed[step, e] = total
        for side in sides:
            @pl.when(has_slab[side])
            def _(side=side):
                slab_copy(step, side, e).start()

    def store(e):
        return pltpu.make_async_copy(out.at[e], out_hbm.at[real(e)], store_sem.at[e])

    def two(lhs, rhs, contract):
        both = dot(lhs, rhs[0], contract)
        m = both.shape[0] // 2
        return both[:m] + both[m:] + dot(lhs[:m], rhs[1], contract)

    def solve(step, e):
        for side in sides:
            @pl.when(has_slab[side])
            def _(side=side):
                slab_copy(step, 1 - side, e).wait_recv()
        rights = []
        for j, block in enumerate((rim[step, 0, e], mixed[step, e], rim[step, 1, e])):
            hi, lo = split(block.reshape(2 * size, size))
            half = dot(jnp.concatenate([hi, lo], 1), c_right[j], 1)
            half = half[:, :size] + half[:, size:]
            rights.append(jnp.concatenate([half[:size], half[size:]], 1))
        sigma = two(c_left[...], split(jnp.concatenate(rights, 0)), 0)
        s_hi, s_lo = split(sigma)
        turned = [jnp.concatenate([v, jnp.concatenate([-v[:, size:], v[:, :size]], 1)], 0) for v in (s_hi, s_lo)]
        product = two(r_left[e], turned, 0)
        p_hi, p_lo = split(product)
        result = two(jnp.concatenate([p_hi, p_lo], 0), (r_right[e, 0], r_right[e, 1]), 1)
        target = out.at[e] if step == ITERS - 1 else middle.at[step, e]
        target[0] = result[:, :size]
        target[1] = result[:, size:]
        if step == ITERS - 1:
            store(e).start()

    for step in range(ITERS):
        for i in range(energies + LAG):
            if i < energies:
                for role in roles:
                    when(role.when, lambda role=role: mix(role, step, role.order[step][i]))
            at = i - LAG
            if at < 0:
                continue
            ahead = at - energies + POLLS + 1
            if step < ITERS - 1 and ahead > 0:
                for role in roles:
                    if role.forwards:
                        side = role.forwards[0]
                        when(role.when, lambda: await_halo(
                            role, step + 1, side, min(ahead, len(role.arrivals[step + 1][side]))))
            e = roles[-1].order[step][at]
            if len(roles) > 1:
                e = jnp.where(roles[0].when, roles[0].order[step][at], e)
            solve(step, e)
            if step < ITERS - 1:
                for role in roles:
                    when(role.when, lambda role=role: pass_on(role, step + 1, role.order[step][:at + 1]))
        for role in roles:
            def rest(role=role):
                for side, order in role.arrivals[step].items():
                    await_halo(role, step, side, len(order))
            when(role.when, rest)

    for e in range(energies):
        store(e).wait()
    for step in range(ITERS):
        for role in roles:
            def finish(role=role):
                for lane, (flag, to, orders, side) in enumerate(role.sends):
                    def wait(lane=lane, to=to, order=orders[step], side=side):
                        for e in order:
                            energy_copy(step, lane, source(step, e), to, side, e).wait_send()
                    when(flag, wait)
                if role.forwards:
                    for slot in role.forwards[2]:
                        energy_copy(
                            step, 1, halo.at[step, 1, slot], role.forwards[1], 1, energies - 1 - slot).wait_send()
            when(role.when, finish)
        for side in sides:
            @pl.when(has_slab[side])
            def _(side=side):
                for e in range(energies):
                    slab_copy(step, side, e).wait_send()


def solution(mesh):
    counts = (mesh.shape["energy"], mesh.shape["slab"])

    def local(green_init, retarded, coupling_on, coupling_lower, coupling_upper, phonon_weights):
        current = green_init[:, 0]
        local_ret = retarded[:, 0]
        energies, _, size, _ = current.shape
        block = (2, size, size)
        hbm = pl.BlockSpec(memory_space=pltpu.HBM)
        dma = pltpu.SemaphoreType.DMA
        result = pl.pallas_call(
            functools.partial(kernel, counts),
            out_shape=jax.ShapeDtypeStruct(current.shape, F32),
            in_specs=[hbm] * 6,
            out_specs=hbm,
            scratch_shapes=[
                pltpu.SMEM(phonon_weights.shape, F32),
                pltpu.VMEM(current.shape, F32),
                pltpu.VMEM(current.shape, F32),
                pltpu.VMEM(coupling_on.shape, F32),
                pltpu.VMEM(coupling_on.shape, F32),
                pltpu.VMEM(coupling_on.shape, F32),
                pltpu.VMEM(current.shape, F32),
                dma((6,)),
                dma((energies,)),
                pltpu.VMEM((ITERS, 2, energies) + block, F32),
                pltpu.VMEM((ITERS, 2, energies) + block, F32),
                pltpu.VMEM((ITERS, energies) + block, F32),
                pltpu.VMEM((ITERS - 1, energies) + block, F32),
                pltpu.VMEM((3, 2 * size, 2 * size), BF16),
                pltpu.VMEM((2 * size, 3 * size), BF16),
                pltpu.VMEM((energies, 2 * size, 2 * size), BF16),
                pltpu.VMEM((energies, 2, 2 * size, 2 * size), BF16),
                dma((ITERS, 2, energies)),
                dma((ITERS, 2, energies)),
                dma((ITERS, 2, energies)),
                dma((ITERS, 2, energies)),
            ],
            compiler_params=pltpu.CompilerParams(
                collective_id=0, has_side_effects=True),
        )(phonon_weights, current, local_ret, coupling_on, coupling_lower, coupling_upper)
        return result[:, None]

    in_specs = (
        P("energy", "slab", None, None, None),
        P("energy", "slab", None, None, None),
        P("slab", None, None),
        P("slab", None, None),
        P("slab", None, None),
        P(),
    )
    out_specs = P("energy", "slab", None, None, None)
    return jax.shard_map(local, mesh=mesh, in_specs=in_specs, out_specs=out_specs, check_vma=False)
```

```python
import functools

import jax
import jax.numpy as jnp
from jax import lax
from jax.experimental import pallas as pl
from jax.experimental.pallas import tpu as pltpu
from jax.sharding import PartitionSpec as P

SHIFT_NEAR = 3
SHIFT_FAR = 7
ITERS = 2

LAG = 2
POLLS = 4

MESH = pl.DeviceIdType.MESH
F32 = jnp.float32
BF16 = jnp.bfloat16


def split(x):
    hi = x.astype(BF16)
    lo = (x - hi.astype(F32)).astype(BF16)
    return hi, lo


def dot(a, b, rhs_contract=0):
    return lax.dot_general(a, b, (((1,), (rhs_contract,)), ((), ())), preferred_element_type=F32)


def needs(e, count):
    found = []
    for shift in (-SHIFT_FAR, -SHIFT_NEAR, SHIFT_NEAR, SHIFT_FAR):
        if e - shift < 0:
            found.append((0, e - shift + count))
        elif e - shift >= count:
            found.append((1, e - shift - count))
    return found


def by_arrival(count, arrivals, lead=0):
    def ready(e):
        return max(
            [arrivals[side].index(p) - (0 if side else lead) for side, p in needs(e, count) if side in arrivals],
            default=-count)

    return sorted(range(count), key=lambda e: (ready(e), -e))


def inner_first(count):
    half = count // 2
    return list(range(half, count)) + list(range(half - 1, -1, -1))


class Role:
    def __init__(self, when, order, arrivals, sends, forwards=None):
        self.when, self.order, self.arrivals = when, order, arrivals
        self.sends, self.forwards = sends, forwards
        self.waited, self.sent = {}, {}


def kernel(
    counts, weights_in, green_in, retarded_in, on_in, low_in, up_in, out_hbm,
    weights, green, retarded, c_on, c_low, c_up, out, load_sem, store_sem,
    halo, rim, mixed, middle, c_right, c_left, r_left, r_right,
    e_send, e_recv, s_send, s_recv, detour, t_send, t_recv,
):
    n_energy, n_slab = counts
    energies, _, size, _ = green.shape
    d = lax.axis_index("energy")
    s = lax.axis_index("slab")
    sides = (0, 1)
    has_slab = (s > 0, s < n_slab - 1)
    square = n_energy == 4
    upper = inner_first(energies)
    to_right = [e for e in upper if e >= energies - SHIFT_FAR]
    to_left = [energies - 1 - e for e in to_right]

    if square:
        flip = d >= 2
        is_end = jnp.logical_or(d == 0, d == n_energy - 1)
        is_mid = jnp.logical_not(is_end)
        x_peer = {"energy": d + 1 - 2 * (d % 2)}
        y_peer = {"energy": d + 2 - 4 * (d // 2)}
        peers = [(None, x_peer), (None, y_peer)]
        half = energies // 2
        extra = [e for e in to_left if e not in to_right]
        start = to_right[:2] + to_right[-1:] + to_right[2:-1]
        later = [to_right[0]] + to_right[half - 1:half + 1] + to_right[1:half - 1] + to_right[half + 1:]
        mid_send = [start + extra] + [later + extra] * (ITERS - 1)
        end_arrivals = [{1: order} for order in mid_send]
        end_order = [by_arrival(energies, arrivals) for arrivals in end_arrivals]
        end_send = [start] + [[e for e in order if e in to_right] for order in end_order[:-1]]
        mid_arrivals = [
            {0: own, 1: [energies - 1 - e for e in order if e in to_right]}
            for own, order in zip(end_send, mid_send)]
        mid_order = [by_arrival(energies, arrivals, 2.5 if step else 1.5) for step, arrivals in enumerate(mid_arrivals)]
        roles = [
            Role(is_end, end_order, end_arrivals, [(None, x_peer, end_send, 0)], (1, y_peer, to_right)),
            Role(is_mid, mid_order, mid_arrivals, [(None, x_peer, mid_send, 1)]),
        ]
        empty = [(is_end, 0)]
        have = {}
    else:
        flip = None
        left, right = {"energy": d - 1}, {"energy": d + 1}
        has_left, has_right = d > 0, d < n_energy - 1
        peers = [(has_left, left), (has_right, right)]
        arrivals = {0: to_right, 1: to_left}
        every = range(ITERS)
        roles = [Role(
            None, [by_arrival(energies, arrivals) for _ in every], [arrivals for _ in every],
            [(has_left, left, [to_left for _ in every], 1), (has_right, right, [to_right for _ in every], 0)])]
        empty = [(jnp.logical_not(has_left), 0), (jnp.logical_not(has_right), 1)]
        have = {0: has_left, 1: has_right}

    def when(flag, body):
        if flag is None:
            body()
        else:
            pl.when(flag)(body)

    def real(e):
        return e if flip is None else jnp.where(flip, energies - 1 - e, e)

    loads = [
        pltpu.make_async_copy(src, dst, load_sem.at[i])
        for i, (src, dst) in enumerate((
            (low_in, c_low), (on_in, c_on), (up_in, c_up), (retarded_in, retarded),
            (weights_in, weights), (green_in, green)))]

    slabs = [(has_slab[0], {"slab": s - 1}), (has_slab[1], {"slab": s + 1})]
    barrier = pltpu.get_barrier_semaphore()
    total = 0
    for flag, to in peers + slabs:
        def greet(to=to):
            pl.semaphore_signal(barrier, inc=1, device_id=to, device_id_type=MESH)
        when(flag, greet)
        total = total + (1 if flag is None else jnp.where(flag, 1, 0))
    pl.semaphore_wait(barrier, total)

    def held(step, e):
        return green.at[real(e)] if step == 0 else middle.at[step - 1, e]

    def source(step, e):
        return green_in.at[real(e)] if step == 0 else middle.at[step - 1, e]

    def energy_copy(step, lane, src, to, side, slot, half=False):
        dst = halo.at[step, side, slot]
        if half:
            src, dst = src.at[0], dst.at[0]
        return pltpu.make_async_remote_copy(
            src_ref=src, dst_ref=dst,
            send_sem=e_send.at[step, lane, slot], recv_sem=e_recv.at[step, side, slot],
            device_id=to, device_id_type=MESH,
        )

    def detour_out(step):
        return pltpu.make_async_remote_copy(
            src_ref=source(step, energies - 1).at[1], dst_ref=detour.at[step],
            send_sem=t_send.at[step, 0], recv_sem=t_recv.at[step, 0],
            device_id=y_peer, device_id_type=MESH,
        )

    def detour_on(step):
        return pltpu.make_async_remote_copy(
            src_ref=detour.at[step], dst_ref=halo.at[step, 1, 0, 1],
            send_sem=t_send.at[step, 1], recv_sem=t_recv.at[step, 1],
            device_id=x_peer, device_id_type=MESH,
        )

    def relay_detour(step):
        if square:
            @pl.when(is_end)
            def _():
                detour_out(step).wait_recv()
                detour_on(step).start()

    def slab_copy(step, side, e):
        return pltpu.make_async_remote_copy(
            src_ref=mixed.at[step, e], dst_ref=rim.at[step, 1 - side, e],
            send_sem=s_send.at[step, side, e], recv_sem=s_recv.at[step, 1 - side, e],
            device_id=slabs[side][1], device_id_type=MESH,
        )

    def pass_on(role, step, done):
        for lane, (flag, to, orders, side) in enumerate(role.sends):
            order = orders[step]
            start = stop = role.sent.get((step, lane), 0)
            while stop < len(order) and order[stop] in done:
                stop += 1

            def send(lane=lane, to=to, todo=order[start:stop], side=side):
                for e in todo:
                    half = square and side == 1 and e == energies - 1
                    energy_copy(step, lane, source(step, e), to, side, e, half).start()
                    if half:
                        detour_out(step).start()
            if stop > start:
                when(flag, send)
            role.sent[step, lane] = stop

    def await_halo(role, step, side, upto):
        start = role.waited.get((step, side), 0)
        if upto <= start:
            return
        role.waited[step, side] = upto

        def wait():
            for slot in role.arrivals[step][side][start:upto]:
                block = halo.at[step, side, slot]
                last = energies - 1 if role.forwards else 0
                half = square and side == 1 and slot == last
                energy_copy(step, 0, block, peers[0][1], side, slot, half).wait_recv()
                if half and not role.forwards:
                    detour_on(step).wait_recv()
                if role.forwards and role.forwards[0] == side and slot in role.forwards[2]:
                    energy_copy(step, 1, block, role.forwards[1], 1, energies - 1 - slot, half).start()
        when(have.get(side), wait)

    for role in roles:
        when(role.when, lambda role=role: pass_on(role, 0, range(energies)))

    for load in loads:
        load.start()

    for flag, side in empty:
        @pl.when(flag)
        def _(side=side):
            halo[:, side] = jnp.zeros_like(halo[:, side])

    for side in sides:
        @pl.when(jnp.logical_not(has_slab[side]))
        def _(side=side):
            rim[:, side] = jnp.zeros_like(rim[:, side])

    for load in loads[:3]:
        load.wait()
    highs, lows = [], []
    for j, ref in enumerate((c_low, c_on, c_up)):
        hi, lo = split(ref[0])
        c_right[j] = jnp.concatenate(
            [jnp.concatenate([hi, hi], 1), jnp.concatenate([lo, lo], 1)], 0)
        highs.append(hi)
        lows.append(lo)
    c_left[...] = jnp.concatenate([jnp.concatenate(highs, 1), jnp.concatenate(lows, 1)], 0)

    loads[3].wait()

    @pl.loop(0, energies)
    def _(e):
        re_hi, re_lo = split(retarded[real(e), 0])
        im_hi, im_lo = split(retarded[real(e), 1])
        top_hi = jnp.concatenate([re_hi, im_hi], 1)
        top_lo = jnp.concatenate([re_lo, im_lo], 1)
        r_left[e] = jnp.concatenate([top_hi, top_lo], 0)
        r_right[e, 0] = jnp.concatenate([top_hi, jnp.concatenate([-im_hi, re_hi], 1)], 0)
        r_right[e, 1] = jnp.concatenate([top_lo, jnp.concatenate([-im_lo, re_lo], 1)], 0)

    for load in loads[4:]:
        load.wait()
    shares = [weights[k] if flip is None else jnp.where(flip, weights[3 - k], weights[k]) for k in range(4)]

    def part(step, e):
        if e < 0:
            return halo[step, 0, e + energies]
        if e >= energies:
            return halo[step, 1, e - energies]
        return held(step, e)[...]

    def mix(role, step, e):
        for side, slot in needs(e, energies):
            if side in role.arrivals[step]:
                await_halo(role, step, side, role.arrivals[step][side].index(slot) + 1)
        total = shares[0] * part(step, e + SHIFT_FAR)
        total = total + shares[1] * part(step, e + SHIFT_NEAR)
        total = total + shares[2] * part(step, e - SHIFT_NEAR)
        total = total + shares[3] * part(step, e - SHIFT_FAR)
        mixed[step, e] = total
        for side in sides:
            @pl.when(has_slab[side])
            def _(side=side):
                slab_copy(step, side, e).start()

    def store(e):
        return pltpu.make_async_copy(out.at[e], out_hbm.at[real(e)], store_sem.at[e])

    def two(lhs, rhs, contract):
        both = dot(lhs, rhs[0], contract)
        m = both.shape[0] // 2
        return both[:m] + both[m:] + dot(lhs[:m], rhs[1], contract)

    def solve(step, e):
        for side in sides:
            @pl.when(has_slab[side])
            def _(side=side):
                slab_copy(step, 1 - side, e).wait_recv()
        rights = []
        for j, block in enumerate((rim[step, 0, e], mixed[step, e], rim[step, 1, e])):
            hi, lo = split(block.reshape(2 * size, size))
            half = dot(jnp.concatenate([hi, lo], 1), c_right[j], 1)
            half = half[:, :size] + half[:, size:]
            rights.append(jnp.concatenate([half[:size], half[size:]], 1))
        sigma = two(c_left[...], split(jnp.concatenate(rights, 0)), 0)
        s_hi, s_lo = split(sigma)
        turned = [jnp.concatenate([v, jnp.concatenate([-v[:, size:], v[:, :size]], 1)], 0) for v in (s_hi, s_lo)]
        product = two(r_left[e], turned, 0)
        p_hi, p_lo = split(product)
        result = two(jnp.concatenate([p_hi, p_lo], 0), (r_right[e, 0], r_right[e, 1]), 1)
        target = out.at[e] if step == ITERS - 1 else middle.at[step, e]
        target[0] = result[:, :size]
        target[1] = result[:, size:]
        if step == ITERS - 1:
            store(e).start()

    for step in range(ITERS):
        for i in range(energies + LAG):
            if i < energies:
                for role in roles:
                    when(role.when, lambda role=role: mix(role, step, role.order[step][i]))
            if step == 0 and i == 0:
                relay_detour(step)
            at = i - LAG
            if at < 0:
                continue
            ahead = at - energies + POLLS + 1
            if step < ITERS - 1 and ahead == 1:
                relay_detour(step + 1)
            if step < ITERS - 1 and ahead > 0:
                for role in roles:
                    if role.forwards:
                        side = role.forwards[0]
                        when(role.when, lambda: await_halo(
                            role, step + 1, side, min(ahead, len(role.arrivals[step + 1][side]))))
            e = roles[-1].order[step][at]
            if len(roles) > 1:
                e = jnp.where(roles[0].when, roles[0].order[step][at], e)
            solve(step, e)
            if step < ITERS - 1:
                for role in roles:
                    when(role.when, lambda role=role: pass_on(role, step + 1, role.order[step][:at + 1]))
        for role in roles:
            def rest(role=role):
                for side, order in role.arrivals[step].items():
                    await_halo(role, step, side, len(order))
            when(role.when, rest)

    for e in range(energies):
        store(e).wait()
    for step in range(ITERS):
        for role in roles:
            def finish(role=role):
                for lane, (flag, to, orders, side) in enumerate(role.sends):
                    def wait(lane=lane, to=to, order=orders[step], side=side):
                        for e in order:
                            half = square and side == 1 and e == energies - 1
                            energy_copy(step, lane, source(step, e), to, side, e, half).wait_send()
                            if half:
                                detour_out(step).wait_send()
                    when(flag, wait)
                if role.forwards:
                    for slot in role.forwards[2]:
                        energy_copy(
                            step, 1, halo.at[step, 1, slot], role.forwards[1], 1, energies - 1 - slot,
                            slot == energies - 1).wait_send()
                    detour_on(step).wait_send()
            when(role.when, finish)
        for side in sides:
            @pl.when(has_slab[side])
            def _(side=side):
                for e in range(energies):
                    slab_copy(step, side, e).wait_send()


def solution(mesh):
    counts = (mesh.shape["energy"], mesh.shape["slab"])

    def local(green_init, retarded, coupling_on, coupling_lower, coupling_upper, phonon_weights):
        current = green_init[:, 0]
        local_ret = retarded[:, 0]
        energies, _, size, _ = current.shape
        block = (2, size, size)
        hbm = pl.BlockSpec(memory_space=pltpu.HBM)
        dma = pltpu.SemaphoreType.DMA
        result = pl.pallas_call(
            functools.partial(kernel, counts),
            out_shape=jax.ShapeDtypeStruct(current.shape, F32),
            in_specs=[hbm] * 6,
            out_specs=hbm,
            scratch_shapes=[
                pltpu.SMEM(phonon_weights.shape, F32),
                pltpu.VMEM(current.shape, F32),
                pltpu.VMEM(current.shape, F32),
                pltpu.VMEM(coupling_on.shape, F32),
                pltpu.VMEM(coupling_on.shape, F32),
                pltpu.VMEM(coupling_on.shape, F32),
                pltpu.VMEM(current.shape, F32),
                dma((6,)),
                dma((energies,)),
                pltpu.VMEM((ITERS, 2, energies) + block, F32),
                pltpu.VMEM((ITERS, 2, energies) + block, F32),
                pltpu.VMEM((ITERS, energies) + block, F32),
                pltpu.VMEM((ITERS - 1, energies) + block, F32),
                pltpu.VMEM((3, 2 * size, 2 * size), BF16),
                pltpu.VMEM((2 * size, 3 * size), BF16),
                pltpu.VMEM((energies, 2 * size, 2 * size), BF16),
                pltpu.VMEM((energies, 2, 2 * size, 2 * size), BF16),
                dma((ITERS, 2, energies)),
                dma((ITERS, 2, energies)),
                dma((ITERS, 2, energies)),
                dma((ITERS, 2, energies)),
                pltpu.VMEM((ITERS, size, size), F32),
                dma((ITERS, 2)),
                dma((ITERS, 2)),
            ],
            compiler_params=pltpu.CompilerParams(
                collective_id=0, has_side_effects=True),
        )(phonon_weights, current, local_ret, coupling_on, coupling_lower, coupling_upper)
        return result[:, None]

    in_specs = (
        P("energy", "slab", None, None, None),
        P("energy", "slab", None, None, None),
        P("slab", None, None),
        P("slab", None, None),
        P("slab", None, None),
        P(),
    )
    out_specs = P("energy", "slab", None, None, None)
    return jax.shard_map(local, mesh=mesh, in_specs=in_specs, out_specs=out_specs, check_vma=False)
```
